32 devices in a mesh: px: 8 (over z, y), py: 4 (over x, core).
Axes of the slice: x: 2, y: 2, z: 4, core: 2. Of those that a mesh axis runs over, the one named last changes fastest.
Arguments:
- measured: float32 [256, 128, 128], P('px', 'py'), may hold values from -432 to 432, as said below
- spread_function: float32 [8, 8, 16], replicated, may hold values from 0.01 to 1
- smoothing: float32 [1], replicated, may hold values from 0.1 to 0.4
Outputs:
- solution_field: float32 [256, 128, 128], P('px', 'py')
- residual: float32 [256, 128, 128], P('px', 'py')
The draws below stay inside these ranges and needn't reach their ends.
Inputs may be any that keep to these rules, and one draw needn't show every extreme that they name: measured is a float32 volume whose entries lie within the stated bounds.
All inputs are finite; a program needn't handle non-finite values.
Results may differ from the reference program's by a relative error of at most 0.0003.
Values sent between devices are 32-bit elements.
A program may use at most 128 MiB of HBM per device.

```python
import math
import jax
import jax.numpy as jnp

NZ = 128
PSX = 8
PSY = 8
PSZ = 16
ITERS = 5
NX = 256
NY = 128


def draw_measured(key, part):
    noise_key, row_key, column_key = jax.random.split(key, 3)
    noise = jnp.clip(jax.random.normal(noise_key, (NX, NY, NZ), jnp.float32), -6.0, 6.0)
    rows = jax.random.uniform(row_key, (NX, 1, 1), jnp.float32, 0.2, 3.0)
    columns = jax.random.uniform(column_key, (1, NY, 1), jnp.float32, 0.2, 3.0)
    return 8.0 * noise * rows * columns


def setup_inputs(seed: int = 0) -> dict:
    splits = jax.random.split(jax.random.key(seed), 4)
    measured = draw_measured(jax.random.fold_in(splits[3], 71), 0)
    spread_function = jnp.clip(jnp.exp(jax.random.uniform(splits[1], (PSX, PSY, PSZ), jnp.float32, math.log(0.01), math.log(1.0))), 0.01, 1.0)
    smoothing = jnp.clip(jnp.exp(jax.random.uniform(splits[2], (1,), jnp.float32, math.log(0.1), math.log(0.4))), 0.1, 0.4)
    return dict(measured=measured, spread_function=spread_function, smoothing=smoothing)


def stencil(volume):
    padded = jnp.pad(volume, 1)
    beside = padded[2:, 1:-1, 1:-1] + padded[:-2, 1:-1, 1:-1]
    beside = beside + padded[1:-1, 2:, 1:-1] + padded[1:-1, :-2, 1:-1]
    beside = beside + padded[1:-1, 1:-1, 2:] + padded[1:-1, 1:-1, :-2]
    return 6.0 * volume - beside


def reference(measured, spread_function, smoothing):
    penalty = smoothing[0]
    kernel = spread_function / jnp.sum(spread_function)
    placed = jnp.pad(kernel, ((0, NX - PSX), (0, NY - PSY), (0, NZ - PSZ)))
    placed = jnp.roll(placed, (-(PSX // 2), -(PSY // 2), -(PSZ // 2)), axis=(0, 1, 2))
    transfer = jnp.fft.fftn(placed)
    power = jnp.real(transfer) ** 2 + jnp.imag(transfer) ** 2
    right_side = jnp.real(jnp.fft.ifftn(jnp.conj(transfer) * jnp.fft.fftn(measured)))

    def operate(volume):
        filtered = jnp.real(jnp.fft.ifftn(power * jnp.fft.fftn(volume)))
        return filtered + penalty * stencil(volume)

    solution_field = jnp.zeros_like(right_side)
    residual = right_side
    direction = right_side
    norm_now = jnp.sum(residual * residual)
    for count in range(ITERS):
        image = operate(direction)
        alpha = norm_now / jnp.sum(direction * image)
        solution_field = solution_field + alpha * direction
        residual = residual - alpha * image
        fresh = jnp.sum(residual * residual)
        direction = residual + (fresh / norm_now) * direction
        norm_now = fresh
    return solution_field, residual
```

```python
import functools

import jax
import jax.numpy as jnp
import numpy as np
from jax import lax
from jax.experimental import pallas as pl
from jax.experimental.pallas import tpu as pltpu
from jax.sharding import PartitionSpec as P

ITERS = 5
MESH = pl.DeviceIdType.MESH
DIRECTIONS = [(1, 0), (-1, 0), (0, 1), (0, -1), (1, 1), (1, -1), (-1, 1), (-1, -1)]


def round_up(value, unit):
    return -(-value // unit) * unit


def split_table(table):
    table = table.astype(np.float32)
    high = table.astype(jnp.bfloat16)
    low = (table - high.astype(np.float32)).astype(jnp.bfloat16)
    return high, low


def stacked(table):
    high, low = split_table(table)
    return np.concatenate([high, high, low], axis=1)


def make_tables(local_x, local_y, planes, reach_x, reach_y):
    pad_x, pad_y = round_up(reach_x, 8), round_up(reach_y, 8)
    size_x, size_y = local_x + 2 * reach_x, local_y + 2 * reach_y
    ext_x, ext_y = local_x + 2 * pad_x, local_y + 2 * pad_y
    waves_y = round_up(size_y // 2 + 1, 8)

    def forward(ext, size, pad, reach, rows, used):
        spot = np.arange(ext) - (pad - reach)
        inside = (spot >= 0) & (spot < size)
        wave = np.arange(rows)
        angle = 2.0 * np.pi * ((wave[:, None] * spot[None, :]) % size) / size
        mask = inside[None, :] * (wave < used)[:, None]
        return np.cos(angle) * mask, np.sin(angle) * mask

    cos_y, sin_y = forward(ext_y, size_y, pad_y, reach_y, waves_y, size_y // 2 + 1)
    cos_x, sin_x = forward(ext_x, size_x, pad_x, reach_x, ext_x, size_x)
    y_forward = np.concatenate([cos_y, -sin_y], axis=0)
    x_forward = np.concatenate([cos_x, sin_x], axis=0)
    keep_x = slice(pad_x, pad_x + local_x)
    keep_y = slice(pad_y, pad_y + local_y)
    x_inverse = np.concatenate([cos_x[:, keep_x].T, sin_x[:, keep_x].T], axis=0) / size_x
    weight = np.full(waves_y, 2.0)
    weight[0] = 1.0
    if size_y % 2 == 0:
        weight[size_y // 2] = 1.0
    weight = weight[:, None] / size_y
    y_inverse = np.concatenate([(cos_y * weight)[:, keep_y], -(sin_y * weight)[:, keep_y]], axis=0).T
    index = np.arange(planes)
    angle = 2.0 * np.pi * ((index[:, None] * index[None, :]) % planes) / planes
    cos_z, sin_z = np.cos(angle), np.sin(angle)
    z_forward = np.block([[cos_z, -sin_z], [sin_z, cos_z]])
    z_inverse = np.block([[cos_z, sin_z], [-sin_z, cos_z]]) / planes
    lap = (
        6.0
        - 2.0 * np.cos(2.0 * np.pi * np.arange(waves_y) / size_y)[:, None, None]
        - 2.0 * np.cos(2.0 * np.pi * np.arange(ext_x) / size_x)[None, :, None]
        - 2.0 * np.cos(2.0 * np.pi * index / planes)[None, None, :]
    ).reshape(waves_y * ext_x, planes)
    return dict(
        y_forward=stacked(y_forward),
        x_forward=stacked(x_forward),
        x_inverse=stacked(x_inverse),
        y_inverse=stacked(y_inverse),
        z_forward=np.stack(split_table(z_forward)),
        z_inverse=np.stack(split_table(z_inverse)),
        lap=lap.astype(np.float32),
    )


def halves(values):
    high = values.astype(jnp.bfloat16)
    low = (values - high.astype(jnp.float32)).astype(jnp.bfloat16)
    return high, low


def stack_rows(values):
    high, low = halves(values)
    return jnp.concatenate([high, low, high], axis=0)


def dot(left, right):
    return jnp.dot(left, right, preferred_element_type=jnp.float32)


def kernel(
    shape, psf_shape, groups,
    measured, psf, smoothing, y_fwd, x_fwd, x_inv, y_inv, z_fwd, z_inv, lap,
    field, residual,
    blocks, placed, mixed, spectrum, back, image, walk, pull, power, adjoint, sums_y, sums_x,
    send_sem, recv_sem, sum_send, sum_recv,
):
    local_x, local_y, planes = shape
    groups_x, groups_y = groups
    pad_x = (blocks.shape[1] - local_x) // 2
    pad_y = (blocks.shape[2] - local_y) // 2
    ext_x, ext_y = blocks.shape[1], blocks.shape[2]
    waves = y_fwd.shape[0] // 2
    rows = waves * ext_x
    me_x, me_y = lax.axis_index("px"), lax.axis_index("py")
    penalty = smoothing[0]

    def device(step_x, step_y):
        return {
            "px": lax.rem(me_x + step_x + groups_x, groups_x),
            "py": lax.rem(me_y + step_y + groups_y, groups_y),
        }

    barrier = pltpu.get_barrier_semaphore()
    partners = DIRECTIONS + [(0, k) for k in range(1, groups_y)] + [(k, 0) for k in range(1, groups_x)]
    for step in partners:
        pl.semaphore_signal(barrier, inc=1, device_id=device(*step), device_id_type=MESH)

    inner_x, inner_y = pl.ds(pad_x, local_x), pl.ds(pad_y, local_y)

    def span(step, local, pad):
        if step == 0:
            return pl.ds(pad, local), pl.ds(pad, local)
        if step > 0:
            return pl.ds(local, pad), pl.ds(0, pad)
        return pl.ds(pad, pad), pl.ds(pad + local, pad)

    def halo(side):
        copies = []
        for number, (step_x, step_y) in enumerate(DIRECTIONS):
            from_x, to_x = span(step_x, local_x, pad_x)
            from_y, to_y = span(step_y, local_y, pad_y)
            copies.append(
                pltpu.make_async_remote_copy(
                    src_ref=blocks.at[side, from_x, from_y, :],
                    dst_ref=blocks.at[side, to_x, to_y, :],
                    send_sem=send_sem.at[side, number],
                    recv_sem=recv_sem.at[side, number],
                    device_id=device(step_x, step_y),
                    device_id_type=MESH,
                )
            )
        for copy in copies:
            copy.start()
        return copies

    def forward(block):
        @pl.loop(0, ext_x // 8)
        def _(group):
            for k in range(4):
                x = group * 8 + 2 * k
                pair = jnp.concatenate([block[x], block[x + 1]], axis=1)
                out = dot(y_fwd[...], stack_rows(pair))
                mixed[pl.ds(x * 2 * waves, 2 * waves), :] = out[:, :planes]
                mixed[pl.ds((x + 1) * 2 * waves, 2 * waves), :] = out[:, planes:]

        @pl.loop(0, waves // 4)
        def _(group):
            for k in range(4):
                wave = group * 4 + k
                real = mixed[pl.ds(wave, ext_x, stride=2 * waves), :]
                imag = mixed[pl.ds(wave + waves, ext_x, stride=2 * waves), :]
                out = dot(x_fwd[...], stack_rows(jnp.concatenate([real, imag], axis=1)))
                cosine, sine = out[:ext_x], out[ext_x:]
                spectrum[pl.ds(wave * ext_x, ext_x), :planes] = cosine[:, :planes] + sine[:, planes:]
                spectrum[pl.ds(wave * ext_x, ext_x), planes:] = cosine[:, planes:] - sine[:, :planes]

    def along_z(values, table):
        high, low = halves(values)
        return dot(high, table[0]) + dot(low, table[0]) + dot(high, table[1])

    chunk = ext_x * 2

    def apply_filter(by):
        @pl.loop(0, rows // chunk)
        def _(group):
            where = pl.ds(group * chunk, chunk)
            values = along_z(spectrum[where, :], z_fwd)
            real, imag = by(where, values[:, :planes], values[:, planes:])
            spectrum[where, :] = along_z(jnp.concatenate([real, imag], axis=1), z_inv)

    def by_power(where, real, imag):
        return real * power[where, :], imag * power[where, :]

    def by_adjoint(where, real, imag):
        re, im = adjoint[where, :planes], adjoint[where, planes:]
        return real * re + imag * im, imag * re - real * im

    def inverse(store):
        @pl.loop(0, waves // 4)
        def _(group):
            for k in range(4):
                wave = group * 4 + k
                out = dot(x_inv[...], stack_rows(spectrum[pl.ds(wave * ext_x, ext_x), :]))
                cosine, sine = out[:local_x], out[local_x:]
                back[pl.ds(wave * local_x, local_x), :] = cosine[:, :planes] - sine[:, planes:]
                back[pl.ds((wave + waves) * local_x, local_x), :] = cosine[:, planes:] + sine[:, :planes]

        @pl.loop(0, local_x // 8)
        def _(group):
            for k in range(4):
                x = group * 8 + 2 * k
                left = back[pl.ds(x, 2 * waves, stride=local_x), :]
                right = back[pl.ds(x + 1, 2 * waves, stride=local_x), :]
                out = dot(y_inv[...], stack_rows(jnp.concatenate([left, right], axis=1)))
                store(x, out[:, :planes])
                store(x + 1, out[:, planes:])

    def fold(values):
        return jnp.sum(values.reshape(-1, 8, planes), axis=0)

    def total(gamma, delta, side):
        row = lax.broadcasted_iota(jnp.int32, (8, planes), 0)
        tile = jnp.where(
            row == 0,
            jnp.sum(gamma, axis=0, keepdims=True),
            jnp.where(row == 1, jnp.sum(delta, axis=0, keepdims=True), 0.0),
        )
        for slots, mine, count, base in (
            (sums_y, me_y, groups_y, 0),
            (sums_x, me_x, groups_x, groups_y),
        ):
            slots[side, pl.ds(mine, 1)] = tile[None]
            copies = []
            for k in range(1, count):
                copies.append(
                    pltpu.make_async_remote_copy(
                        src_ref=slots.at[side, mine],
                        dst_ref=slots.at[side, mine],
                        send_sem=sum_send.at[side, base + k],
                        recv_sem=sum_recv.at[side, base + k],
                        device_id=device(0, k) if base == 0 else device(k, 0),
                        device_id_type=MESH,
                    )
                )
            for copy in copies:
                copy.start()
            for copy in copies:
                copy.wait_recv()
            tile = jnp.sum(slots[side], axis=0)
            for copy in copies:
                copy.wait_send()
        sums = jnp.sum(tile, axis=1, keepdims=True)
        return sums[0:1], sums[1:2]

    blocks[0, inner_x, inner_y, :] = measured[...]
    placed[...] = jnp.zeros_like(placed)
    count_x, count_y, _ = psf_shape
    unit = psf[...] / jnp.sum(psf[...])
    origin_x, size_x = pad_x - (count_x - 1), local_x + 2 * (count_x - 1)
    origin_y, size_y = pad_y - (count_y - 1), local_y + 2 * (count_y - 1)
    half_x, half_y = count_x // 2, count_y // 2
    for low_x, high_x in ((0, half_x), (half_x, count_x)):
        at_x = origin_x + (low_x - half_x) % size_x
        for low_y, high_y in ((0, half_y), (half_y, count_y)):
            at_y = origin_y + (low_y - half_y) % size_y
            placed[at_x:at_x + high_x - low_x, at_y:at_y + high_y - low_y, :] = unit[low_x:high_x, low_y:high_y]
    pl.semaphore_wait(barrier, len(partners))
    copies = halo(0)
    forward(placed)

    @pl.loop(0, rows // chunk)
    def _(group):
        where = pl.ds(group * chunk, chunk)
        values = along_z(spectrum[where, :], z_fwd)
        adjoint[where, :] = values
        real, imag = values[:, :planes], values[:, planes:]
        power[where, :] = real * real + imag * imag + penalty * lap[where, :]

    for copy in copies:
        copy.wait_recv()
    forward(blocks.at[0])
    apply_filter(by_adjoint)

    def store_right(x, values):
        blocks[1, pad_x + x, inner_y, :] = values

    inverse(store_right)
    for copy in copies:
        copy.wait_send()

    @pl.loop(0, local_x)
    def _(x):
        field[x] = jnp.zeros((local_y, planes), jnp.float32)

    row = lax.broadcasted_iota(jnp.int32, (local_y, planes), 0)
    lane = lax.broadcasted_iota(jnp.int32, (local_y, planes), 1)
    zero = jnp.zeros((1, 1), jnp.float32)
    edge_low_x = jnp.where(me_x == 0, penalty, 0.0)
    edge_high_x = jnp.where(me_x == groups_x - 1, penalty, 0.0)
    face_low_y = jnp.where((row == 0) & (me_y == 0), penalty, 0.0)
    face_high_y = jnp.where((row == local_y - 1) & (me_y == groups_y - 1), penalty, 0.0)
    face_low_z = jnp.where(lane == 0, penalty, 0.0)
    face_high_z = jnp.where(lane == planes - 1, penalty, 0.0)

    alpha_old, gamma_old = None, None
    for count in range(ITERS):
        side = (count + 1) % 2
        copies = halo(side)
        for copy in copies:
            copy.wait_recv()
        forward(blocks.at[side])
        apply_filter(by_power)

        def store_image(x, values):
            image[x] = values

        inverse(store_image)
        image[0] += edge_low_x * blocks[side, pad_x - 1, inner_y, :]
        image[local_x - 1] += edge_high_x * blocks[side, pad_x + local_x, inner_y, :]

        def finish(x, carry):
            gamma, delta = carry
            here = blocks[side, pad_x + x, inner_y, :]
            below = blocks[side, pad_x + x, pl.ds(pad_y - 1, 1), :]
            above = blocks[side, pad_x + x, pl.ds(pad_y + local_y, 1), :]
            value = image[x] + face_low_y * below + face_high_y * above
            value = value + face_low_z * pltpu.roll(here, 1, 1)
            value = value + face_high_z * pltpu.roll(here, planes - 1, 1)
            image[x] = value
            return gamma + fold(here * here), delta + fold(here * value)

        blank = jnp.zeros((8, planes), jnp.float32)
        gamma, delta = total(*lax.fori_loop(0, local_x, finish, (blank, blank)), side)
        for copy in copies:
            copy.wait_send()
        if count == 0:
            beta = zero
            alpha = gamma / delta
        else:
            beta = gamma / gamma_old
            alpha = gamma / (delta - beta * gamma / alpha_old)
        alpha_old, gamma_old = alpha, gamma
        final = count == ITERS - 1

        @pl.loop(0, local_x)
        def _(x):
            here = blocks[side, pad_x + x, inner_y, :]
            if count == 0:
                step, moved = here, image[x]
            else:
                step = here + beta * walk[x]
                moved = image[x] + beta * pull[x]
            field[x] += alpha * step
            after = here - alpha * moved
            if final:
                residual[x] = after
            else:
                walk[x] = step
                pull[x] = moved
                blocks[1 - side, pad_x + x, inner_y, :] = after


def shards(measured, spread_function, smoothing):
    local_x, local_y, planes = measured.shape
    count_x, count_y, count_z = spread_function.shape
    groups_x, groups_y = lax.axis_size("px"), lax.axis_size("py")
    tables = make_tables(local_x, local_y, planes, count_x - 1, count_y - 1)
    pad_x, pad_y = round_up(count_x - 1, 8), round_up(count_y - 1, 8)
    ext_x, ext_y = local_x + 2 * pad_x, local_y + 2 * pad_y
    waves = tables["y_forward"].shape[0] // 2
    along = jnp.pad(spread_function, ((0, 0), (0, 0), (0, planes - count_z)))
    along = jnp.roll(along, -(count_z // 2), axis=2)
    f32 = jnp.float32
    vmem = pl.BlockSpec(memory_space=pltpu.VMEM)
    body = functools.partial(
        kernel, (local_x, local_y, planes), spread_function.shape, (groups_x, groups_y)
    )
    local = (local_x, local_y, planes)
    return pl.pallas_call(
        body,
        out_shape=[jax.ShapeDtypeStruct(local, f32)] * 2,
        in_specs=[vmem, vmem, pl.BlockSpec(memory_space=pltpu.SMEM)] + [vmem] * 7,
        out_specs=[vmem, vmem],
        scratch_shapes=[
            pltpu.VMEM((2, ext_x, ext_y, planes), f32),
            pltpu.VMEM((ext_x, ext_y, planes), f32),
            pltpu.VMEM((ext_x * 2 * waves, planes), f32),
            pltpu.VMEM((waves * ext_x, 2 * planes), f32),
            pltpu.VMEM((2 * waves * local_x, planes), f32),
            pltpu.VMEM(local, f32),
            pltpu.VMEM(local, f32),
            pltpu.VMEM(local, f32),
            pltpu.VMEM((waves * ext_x, planes), f32),
            pltpu.VMEM((waves * ext_x, 2 * planes), f32),
            pltpu.VMEM((2, groups_y, 8, planes), f32),
            pltpu.VMEM((2, groups_x, 8, planes), f32),
            pltpu.SemaphoreType.DMA((2, len(DIRECTIONS))),
            pltpu.SemaphoreType.DMA((2, len(DIRECTIONS))),
            pltpu.SemaphoreType.DMA((2, groups_x + groups_y)),
            pltpu.SemaphoreType.DMA((2, groups_x + groups_y)),
        ],
        compiler_params=pltpu.CompilerParams(
            collective_id=0, has_side_effects=True, vmem_limit_bytes=48 * 1024 * 1024
        ),
    )(
        measured, along, smoothing,
        *[jnp.asarray(tables[name]) for name in (
            "y_forward", "x_forward", "x_inverse", "y_inverse", "z_forward", "z_inverse", "lap"
        )],
    )


def solution(mesh):
    return jax.shard_map(
        shards,
        mesh=mesh,
        in_specs=(P("px", "py", None), P(), P()),
        out_specs=(P("px", "py", None), P("px", "py", None)),
        check_vma=False,
    )
```

```python
import functools

import jax
import jax.numpy as jnp
import numpy as np
from jax import lax
from jax.experimental import pallas as pl
from jax.experimental.pallas import tpu as pltpu
from jax.sharding import PartitionSpec as P

ITERS = 5
MESH = pl.DeviceIdType.MESH
DIRECTIONS = [(1, 0), (-1, 0), (0, 1), (0, -1), (1, 1), (1, -1), (-1, 1), (-1, -1)]


def round_up(value, unit):
    return -(-value // unit) * unit


def split_table(table):
    table = table.astype(np.float32)
    high = table.astype(jnp.bfloat16)
    low = (table - high.astype(np.float32)).astype(jnp.bfloat16)
    return high, low


def stacked(table):
    high, low = split_table(table)
    return np.concatenate([high, low, high, low, high], axis=1)


def make_tables(local_x, local_y, planes, reach_x, reach_y):
    pad_x, pad_y = round_up(reach_x, 8), round_up(reach_y, 8)
    size_x, size_y = local_x + 2 * reach_x, local_y + 2 * reach_y
    ext_x, ext_y = local_x + 2 * pad_x, local_y + 2 * pad_y
    waves_y = round_up(size_y // 2 + 1, 8)

    def forward(ext, size, pad, reach, rows, used):
        spot = np.arange(ext) - (pad - reach)
        inside = (spot >= 0) & (spot < size)
        wave = np.arange(rows)
        angle = 2.0 * np.pi * ((wave[:, None] * spot[None, :]) % size) / size
        mask = inside[None, :] * (wave < used)[:, None]
        return np.cos(angle) * mask, np.sin(angle) * mask

    cos_y, sin_y = forward(ext_y, size_y, pad_y, reach_y, waves_y, size_y // 2 + 1)
    cos_x, sin_x = forward(ext_x, size_x, pad_x, reach_x, ext_x, size_x)
    y_forward = np.concatenate([cos_y, -sin_y], axis=0)
    x_forward = np.concatenate([cos_x, sin_x], axis=0)
    keep_x = slice(pad_x, pad_x + local_x)
    keep_y = slice(pad_y, pad_y + local_y)
    x_inverse = np.concatenate([cos_x[:, keep_x].T, sin_x[:, keep_x].T], axis=0) / size_x
    weight = np.full(waves_y, 2.0)
    weight[0] = 1.0
    if size_y % 2 == 0:
        weight[size_y // 2] = 1.0
    weight = weight[:, None] / size_y
    y_inverse = np.concatenate([(cos_y * weight)[:, keep_y], -(sin_y * weight)[:, keep_y]], axis=0).T
    index = np.arange(planes)
    angle = 2.0 * np.pi * ((index[:, None] * index[None, :]) % planes) / planes
    cos_z, sin_z = np.cos(angle), np.sin(angle)
    z_forward = np.block([[cos_z, -sin_z], [sin_z, cos_z]])
    z_inverse = np.block([[cos_z, sin_z], [-sin_z, cos_z]]) / planes
    lap = (
        6.0
        - 2.0 * np.cos(2.0 * np.pi * np.arange(waves_y) / size_y)[:, None, None]
        - 2.0 * np.cos(2.0 * np.pi * np.arange(ext_x) / size_x)[None, :, None]
        - 2.0 * np.cos(2.0 * np.pi * index / planes)[None, None, :]
    ).reshape(waves_y * ext_x, planes)
    return dict(
        y_forward=stacked(y_forward),
        x_forward=stacked(x_forward),
        x_inverse=stacked(x_inverse),
        y_inverse=stacked(y_inverse),
        z_forward=np.stack(split_table(z_forward)),
        z_inverse=np.stack(split_table(z_inverse)),
        lap=lap.astype(np.float32),
    )


def thirds(values):
    high = values.astype(jnp.bfloat16)
    rest = values - high.astype(jnp.float32)
    middle = rest.astype(jnp.bfloat16)
    return high, middle, (rest - middle.astype(jnp.float32)).astype(jnp.bfloat16)


def stack_rows(values):
    high, middle, low = thirds(values)
    return jnp.concatenate([high, high, middle, middle, low], axis=0)


def dot(left, right):
    return jnp.dot(left, right, preferred_element_type=jnp.float32)


def kernel(
    shape, psf_shape, groups,
    measured, psf, smoothing, y_fwd, x_fwd, x_inv, y_inv, z_fwd_far, z_inv_far, lap_far,
    field, residual,
    blocks, placed, mixed, spectrum, back, image, walk, pull, power, adjoint, sums_y, sums_x,
    swing, unit, z_fwd, z_inv, lap,
    send_sem, recv_sem, sum_send, sum_recv, load_sem,
):
    local_x, local_y, planes = shape
    groups_x, groups_y = groups
    pad_x = (blocks.shape[1] - local_x) // 2
    pad_y = (blocks.shape[2] - local_y) // 2
    ext_x, ext_y = blocks.shape[1], blocks.shape[2]
    waves = y_fwd.shape[0] // 2
    rows = waves * ext_x
    me_x, me_y = lax.axis_index("px"), lax.axis_index("py")
    penalty = smoothing[0]
    count_x, count_y, count_z = psf_shape
    reach_x = count_x - 1

    def device(step_x, step_y):
        return {
            "px": lax.rem(me_x + step_x + groups_x, groups_x),
            "py": lax.rem(me_y + step_y + groups_y, groups_y),
        }

    barrier = pltpu.get_barrier_semaphore()
    partners = DIRECTIONS + [(0, k) for k in range(1, groups_y)] + [(k, 0) for k in range(1, groups_x)]
    for step in partners:
        pl.semaphore_signal(barrier, inc=1, device_id=device(*step), device_id_type=MESH)

    inner_x, inner_y = pl.ds(pad_x, local_x), pl.ds(pad_y, local_y)
    loads = [
        pltpu.make_async_copy(far, near, load_sem.at[number])
        for number, (far, near) in enumerate((
            (measured, blocks.at[0, inner_x, inner_y, :]),
            (z_fwd_far, z_fwd), (lap_far, lap), (z_inv_far, z_inv),
        ))
    ]
    for load in loads:
        load.start()

    def span(step, local, pad, width):
        if step == 0:
            return pl.ds(pad, local), pl.ds(pad, local)
        if step > 0:
            return pl.ds(pad + local - width, width), pl.ds(pad - width, width)
        return pl.ds(pad, width), pl.ds(pad + local, width)

    def halo(side, across):
        copies = []
        for number, (step_x, step_y) in enumerate(DIRECTIONS):
            if (step_x != 0) != across:
                continue
            from_x, to_x = span(step_x, local_x, pad_x, reach_x)
            from_y, to_y = span(step_y, local_y, pad_y, pad_y)
            copies.append(
                pltpu.make_async_remote_copy(
                    src_ref=blocks.at[side, from_x, from_y, :],
                    dst_ref=blocks.at[side, to_x, to_y, :],
                    send_sem=send_sem.at[side, number],
                    recv_sem=recv_sem.at[side, number],
                    device_id=device(step_x, step_y),
                    device_id_type=MESH,
                )
            )
        for copy in copies:
            copy.start()
        return copies

    def forward(block, beside=(), across=()):
        def lines(group):
            for k in range(4):
                x = group * 8 + 2 * k
                pair = jnp.concatenate([block[x], block[x + 1]], axis=1)
                out = dot(y_fwd[...], stack_rows(pair))
                mixed[pl.ds(x * 2 * waves, 2 * waves), :] = out[:, :planes]
                mixed[pl.ds((x + 1) * 2 * waves, 2 * waves), :] = out[:, planes:]

        for copy in beside:
            copy.wait_recv()
        pl.loop(pad_x // 8, (pad_x + local_x) // 8)(lines)
        for copy in across:
            copy.wait_recv()
        edge = pad_x // 8
        pl.loop(0, edge)(lines)
        pl.loop(ext_x // 8 - edge, ext_x // 8)(lines)

        @pl.loop(0, waves // 4)
        def _(group):
            for k in range(4):
                wave = group * 4 + k
                real = mixed[pl.ds(wave, ext_x, stride=2 * waves), :]
                imag = mixed[pl.ds(wave + waves, ext_x, stride=2 * waves), :]
                out = dot(x_fwd[...], stack_rows(jnp.concatenate([real, imag], axis=1)))
                cosine, sine = out[:ext_x], out[ext_x:]
                spectrum[pl.ds(wave * ext_x, ext_x), :planes] = cosine[:, :planes] + sine[:, planes:]
                spectrum[pl.ds(wave * ext_x, ext_x), planes:] = cosine[:, planes:] - sine[:, :planes]

    def along_z(values, table):
        high, middle, low = thirds(values)
        small = dot(low, table[0]) + dot(middle, table[1])
        return dot(high, table[0]) + (dot(middle, table[0]) + dot(high, table[1]) + small)

    chunk = rows // 2

    def apply_filter(by):
        @pl.loop(0, rows // chunk)
        def _(group):
            where = pl.ds(group * chunk, chunk)
            values = along_z(spectrum[where, :], z_fwd)
            real, imag = by(where, values[:, :planes], values[:, planes:])
            spectrum[where, :] = along_z(jnp.concatenate([real, imag], axis=1), z_inv)

    def by_power(where, real, imag):
        return real * power[where, :], imag * power[where, :]

    def by_adjoint(where, real, imag):
        re, im = adjoint[where, :planes], adjoint[where, planes:]
        return real * re + imag * im, imag * re - real * im

    def inverse(store):
        @pl.loop(0, waves // 4)
        def _(group):
            for k in range(4):
                wave = group * 4 + k
                out = dot(x_inv[...], stack_rows(spectrum[pl.ds(wave * ext_x, ext_x), :]))
                cosine, sine = out[:local_x], out[local_x:]
                back[pl.ds(wave * local_x, local_x), :] = cosine[:, :planes] - sine[:, planes:]
                back[pl.ds((wave + waves) * local_x, local_x), :] = cosine[:, planes:] + sine[:, :planes]

        @pl.loop(0, local_x // 8)
        def _(group):
            for k in range(4):
                x = group * 8 + 2 * k
                left = back[pl.ds(x, 2 * waves, stride=local_x), :]
                right = back[pl.ds(x + 1, 2 * waves, stride=local_x), :]
                out = dot(y_inv[...], stack_rows(jnp.concatenate([left, right], axis=1)))
                store(x, out[:, :planes])
                store(x + 1, out[:, planes:])

    def start_sum(slots, tile, mine, count, base, side):
        slots[side, pl.ds(mine, 1)] = tile[None]
        copies = []
        for k in range(1, count):
            copies.append(
                pltpu.make_async_remote_copy(
                    src_ref=slots.at[side, mine],
                    dst_ref=slots.at[side, mine],
                    send_sem=sum_send.at[side, base + k],
                    recv_sem=sum_recv.at[side, base + k],
                    device_id=device(0, k) if base == 0 else device(k, 0),
                    device_id_type=MESH,
                )
            )
        for copy in copies:
            copy.start()
        return copies

    def end_sum(slots, copies, side):
        for copy in copies:
            copy.wait_recv()
        tile = jnp.sum(slots[side], axis=0)
        for copy in copies:
            copy.wait_send()
        return tile

    def fold(values):
        return jnp.sum(values.reshape(-1, 8, planes), axis=0)

    def pack(gamma, delta):
        line = lax.broadcasted_iota(jnp.int32, (8, planes), 0)
        return jnp.where(
            line == 0,
            jnp.sum(gamma, axis=0, keepdims=True),
            jnp.where(line == 1, jnp.sum(delta, axis=0, keepdims=True), 0.0),
        )

    placed[...] = jnp.zeros_like(placed)
    for side in range(2):
        blocks[side, 0:pad_x - reach_x] = jnp.zeros((pad_x - reach_x, ext_y, planes), jnp.float32)
        blocks[side, ext_x - pad_x + reach_x:ext_x] = jnp.zeros((pad_x - reach_x, ext_y, planes), jnp.float32)
    unit[...] = jnp.zeros_like(unit)
    unit[:, :, 0:count_z] = psf[...] / jnp.sum(psf[...])
    origin_x, size_x = pad_x - (count_x - 1), local_x + 2 * (count_x - 1)
    origin_y, size_y = pad_y - (count_y - 1), local_y + 2 * (count_y - 1)
    half_x, half_y = count_x // 2, count_y // 2
    for low_x in range(count_x):
        at_x = origin_x + (low_x - half_x) % size_x
        turned = pltpu.roll(unit[low_x], planes - count_z // 2, 1)
        for low_y, high_y in ((0, half_y), (half_y, count_y)):
            at_y = origin_y + (low_y - half_y) % size_y
            placed[at_x, at_y:at_y + high_y - low_y, :] = turned[low_y:high_y]
    pl.semaphore_wait(barrier, len(partners))
    loads[0].wait()
    across = halo(0, True)
    beside = halo(0, False)
    forward(placed)
    loads[1].wait()
    loads[2].wait()

    @pl.loop(0, rows // chunk)
    def _(group):
        where = pl.ds(group * chunk, chunk)
        values = along_z(spectrum[where, :], z_fwd)
        adjoint[where, :] = values
        real, imag = values[:, :planes], values[:, planes:]
        power[where, :] = real * real + imag * imag + penalty * lap[where, :]

    loads[3].wait()
    forward(blocks.at[0], beside, across)
    apply_filter(by_adjoint)

    def store_right(x, values):
        blocks[1, pad_x + x, inner_y, :] = values
        residual[x] = values

    inverse(store_right)
    for copy in across + beside:
        copy.wait_send()
    across = halo(1, True)
    beside = halo(1, False)

    row = lax.broadcasted_iota(jnp.int32, (local_y, planes), 0)
    lane = lax.broadcasted_iota(jnp.int32, (local_y, planes), 1)
    edge_low_x = jnp.where(me_x == 0, penalty, 0.0)
    edge_high_x = jnp.where(me_x == groups_x - 1, penalty, 0.0)
    face_low_y = jnp.where((row == 0) & (me_y == 0), penalty, 0.0)
    face_high_y = jnp.where((row == local_y - 1) & (me_y == groups_y - 1), penalty, 0.0)
    face_low_z = jnp.where(lane == 0, penalty, 0.0)
    face_high_z = jnp.where(lane == planes - 1, penalty, 0.0)

    def operate(side, beside, across):
        forward(blocks.at[side], beside, across)
        apply_filter(by_power)

        def store_image(x, values):
            image[x] = values

        inverse(store_image)
        image[0] += edge_low_x * blocks[side, pad_x - 1, inner_y, :]
        image[local_x - 1] += edge_high_x * blocks[side, pad_x + local_x, inner_y, :]
        for copy in beside + across:
            copy.wait_send()

    def faced(side, x, here):
        below = blocks[side, pad_x + x, pl.ds(pad_y - 1, 1), :]
        above = blocks[side, pad_x + x, pl.ds(pad_y + local_y, 1), :]
        value = image[x] + face_low_y * below + face_high_y * above
        value = value + face_low_z * pltpu.roll(here, 1, 1)
        return value + face_high_z * pltpu.roll(here, planes - 1, 1)

    def sweep(low, high, line, carry):
        def some(group, carry):
            for k in range(4):
                carry = line(low + group * 4 + k, carry)
            return carry

        return lax.fori_loop(0, (high - low) // 4, some, carry)

    def sweep_and_send(line, side):
        blank = jnp.zeros((8, planes), jnp.float32)
        carry = sweep(0, pad_x, line, (blank, blank))
        carry = sweep(local_x - pad_x, local_x, line, carry)
        across = halo(side, True)
        carry = sweep(pad_x, local_x - pad_x, line, carry)
        return pack(*carry), across, halo(side, False)

    operate(1, beside, across)

    def first(x, carry):
        gamma, delta = carry
        here = blocks[1, pad_x + x, inner_y, :]
        value = faced(1, x, here)
        blocks[0, pad_x + x, inner_y, :] = value
        return gamma + fold(here * here), delta + fold(here * value)

    tile, across, beside = sweep_and_send(first, 0)

    alpha_old, gamma_old = None, None
    for count in range(ITERS):
        side = count % 2
        final = count == ITERS - 1
        copies = start_sum(sums_y, tile, me_y, groups_y, 0, side)
        tile = end_sum(sums_y, copies, side)
        copies = start_sum(sums_x, tile, me_x, groups_x, groups_y, side)
        if not final:
            operate(side, beside, across)
        sums = jnp.sum(end_sum(sums_x, copies, side), axis=1, keepdims=True)
        gamma, delta = sums[0:1], sums[1:2]
        if count == 0:
            beta = jnp.zeros((1, 1), jnp.float32)
            alpha = gamma / delta
        else:
            beta = gamma / gamma_old
            alpha = gamma / (delta - beta * gamma / alpha_old)
        alpha_old, gamma_old = alpha, gamma
        alpha_all = jnp.broadcast_to(alpha, (local_y, planes))
        beta_all = jnp.broadcast_to(beta, (local_y, planes))

        def line(x, carry):
            held = blocks[side, pad_x + x, inner_y, :]
            here = residual[x]
            if count == 0:
                step, moved = here, held
                field[x] = alpha_all * step
            else:
                step = here + beta_all * walk[x]
                moved = held + beta_all * pull[x]
                field[x] += alpha_all * step
            after = here - alpha_all * moved
            residual[x] = after
            if final:
                return carry
            walk[x] = step
            pull[x] = moved
            turn = faced(side, x, held)
            if count > 0:
                turn = turn + beta_all * swing[x]
            swing[x] = turn
            value = held - alpha_all * turn
            blocks[1 - side, pad_x + x, inner_y, :] = value
            gamma, delta = carry
            return gamma + fold(after * after), delta + fold(after * value)

        if final:
            sweep(0, local_x, line, 0)
        elif count == ITERS - 2:
            blank = jnp.zeros((8, planes), jnp.float32)
            tile = pack(*sweep(0, local_x, line, (blank, blank)))
        else:
            tile, across, beside = sweep_and_send(line, 1 - side)


def shards(measured, spread_function, smoothing):
    local_x, local_y, planes = measured.shape
    count_x, count_y, count_z = spread_function.shape
    groups_x, groups_y = lax.axis_size("px"), lax.axis_size("py")
    tables = make_tables(local_x, local_y, planes, count_x - 1, count_y - 1)
    pad_x, pad_y = round_up(count_x - 1, 8), round_up(count_y - 1, 8)
    ext_x, ext_y = local_x + 2 * pad_x, local_y + 2 * pad_y
    waves = tables["y_forward"].shape[0] // 2
    f32 = jnp.float32
    vmem = pl.BlockSpec(memory_space=pltpu.VMEM)
    far = pl.BlockSpec(memory_space=pltpu.HBM)
    body = functools.partial(
        kernel, (local_x, local_y, planes), spread_function.shape, (groups_x, groups_y)
    )
    local = (local_x, local_y, planes)
    return pl.pallas_call(
        body,
        out_shape=[jax.ShapeDtypeStruct(local, f32)] * 2,
        in_specs=[far, vmem, pl.BlockSpec(memory_space=pltpu.SMEM)] + [vmem] * 4 + [far] * 3,
        out_specs=[vmem, vmem],
        scratch_shapes=[
            pltpu.VMEM((2, ext_x, ext_y, planes), f32),
            pltpu.VMEM((ext_x, ext_y, planes), f32),
            pltpu.VMEM((ext_x * 2 * waves, planes), f32),
            pltpu.VMEM((waves * ext_x, 2 * planes), f32),
            pltpu.VMEM((2 * waves * local_x, planes), f32),
            pltpu.VMEM(local, f32),
            pltpu.VMEM(local, f32),
            pltpu.VMEM(local, f32),
            pltpu.VMEM((waves * ext_x, planes), f32),
            pltpu.VMEM((waves * ext_x, 2 * planes), f32),
            pltpu.VMEM((2, groups_y, 8, planes), f32),
            pltpu.VMEM((2, groups_x, 8, planes), f32),
            pltpu.VMEM(local, f32),
            pltpu.VMEM((count_x, count_y, planes), f32),
            pltpu.VMEM(tables["z_forward"].shape, jnp.bfloat16),
            pltpu.VMEM(tables["z_inverse"].shape, jnp.bfloat16),
            pltpu.VMEM(tables["lap"].shape, f32),
            pltpu.SemaphoreType.DMA((2, len(DIRECTIONS))),
            pltpu.SemaphoreType.DMA((2, len(DIRECTIONS))),
            pltpu.SemaphoreType.DMA((2, groups_x + groups_y)),
            pltpu.SemaphoreType.DMA((2, groups_x + groups_y)),
            pltpu.SemaphoreType.DMA((4,)),
        ],
        compiler_params=pltpu.CompilerParams(
            collective_id=0, has_side_effects=True, vmem_limit_bytes=48 * 1024 * 1024
        ),
    )(
        measured, spread_function, smoothing,
        *[jnp.asarray(tables[name]) for name in (
            "y_forward", "x_forward", "x_inverse", "y_inverse", "z_forward", "z_inverse", "lap"
        )],
    )


def solution(mesh):
    return jax.shard_map(
        shards,
        mesh=mesh,
        in_specs=(P("px", "py", None), P(), P()),
        out_specs=(P("px", "py", None), P("px", "py", None)),
        check_vma=False,
    )
```

```python
import functools

import jax
import jax.numpy as jnp
import numpy as np
from jax import lax
from jax.experimental import pallas as pl
from jax.experimental.pallas import tpu as pltpu
from jax.sharding import PartitionSpec as P

ITERS = 5
MESH = pl.DeviceIdType.MESH
DIRECTIONS = [(1, 0), (-1, 0), (0, 1), (0, -1), (1, 1), (1, -1), (-1, 1), (-1, -1)]


def round_up(value, unit):
    return -(-value // unit) * unit


def split_table(table):
    table = table.astype(np.float32)
    high = table.astype(jnp.bfloat16)
    low = (table - high.astype(np.float32)).astype(jnp.bfloat16)
    return high, low


def stacked(table):
    high, low = split_table(table)
    return np.concatenate([high, low, high, low, high], axis=1)


def make_tables(local_x, local_y, planes, reach_x, reach_y):
    pad_x, pad_y = round_up(reach_x, 8), round_up(reach_y, 8)
    size_x, size_y = local_x + 2 * reach_x, local_y + 2 * reach_y
    ext_x, ext_y = local_x + 2 * pad_x, local_y + 2 * pad_y
    waves_y = round_up(size_y // 2 + 1, 8)

    def forward(ext, size, pad, reach, rows, used):
        spot = np.arange(ext) - (pad - reach)
        inside = (spot >= 0) & (spot < size)
        wave = np.arange(rows)
        angle = 2.0 * np.pi * ((wave[:, None] * spot[None, :]) % size) / size
        mask = inside[None, :] * (wave < used)[:, None]
        return np.cos(angle) * mask, np.sin(angle) * mask

    cos_y, sin_y = forward(ext_y, size_y, pad_y, reach_y, waves_y, size_y // 2 + 1)
    cos_x, sin_x = forward(ext_x, size_x, pad_x, reach_x, ext_x, size_x)
    y_forward = np.concatenate([cos_y, -sin_y], axis=0)
    x_forward = np.concatenate([cos_x, sin_x], axis=0)
    keep_x = slice(pad_x, pad_x + local_x)
    keep_y = slice(pad_y, pad_y + local_y)
    x_inverse = np.concatenate([cos_x[:, keep_x].T, sin_x[:, keep_x].T], axis=0) / size_x
    weight = np.full(waves_y, 2.0)
    weight[0] = 1.0
    if size_y % 2 == 0:
        weight[size_y // 2] = 1.0
    weight = weight[:, None] / size_y
    y_inverse = np.concatenate([(cos_y * weight)[:, keep_y], -(sin_y * weight)[:, keep_y]], axis=0).T
    index = np.arange(planes)
    angle = 2.0 * np.pi * ((index[:, None] * index[None, :]) % planes) / planes
    cos_z, sin_z = np.cos(angle), np.sin(angle)
    z_forward = np.block([[cos_z, -sin_z], [sin_z, cos_z]])
    z_inverse = np.block([[cos_z, sin_z], [-sin_z, cos_z]]) / planes
    lap = (
        6.0
        - 2.0 * np.cos(2.0 * np.pi * np.arange(waves_y) / size_y)[:, None, None]
        - 2.0 * np.cos(2.0 * np.pi * np.arange(ext_x) / size_x)[None, :, None]
        - 2.0 * np.cos(2.0 * np.pi * index / planes)[None, None, :]
    ).reshape(waves_y * ext_x, planes)
    return dict(
        y_forward=stacked(y_forward),
        x_forward=stacked(x_forward),
        x_inverse=stacked(x_inverse),
        y_inverse=stacked(y_inverse),
        z_forward=np.stack(split_table(z_forward)),
        z_inverse=np.stack(split_table(z_inverse)),
        lap=lap.astype(np.float32),
    )


def thirds(values):
    high = values.astype(jnp.bfloat16)
    rest = values - high.astype(jnp.float32)
    middle = rest.astype(jnp.bfloat16)
    return high, middle, (rest - middle.astype(jnp.float32)).astype(jnp.bfloat16)


def stack_rows(values):
    high, middle, low = thirds(values)
    return jnp.concatenate([high, high, middle, middle, low], axis=0)


def dot(left, right):
    return jnp.dot(left, right, preferred_element_type=jnp.float32)


def kernel(
    shape, psf_shape, groups,
    measured, psf, smoothing, y_fwd, x_fwd, x_inv, y_inv, z_fwd_far, z_inv_far, lap_far,
    field, residual,
    blocks, placed, mixed, spectrum, back, image, walk, pull, power, adjoint, sums_y, sums_x,
    swing, unit, z_fwd, z_inv, lap,
    send_sem, recv_sem, sum_send, sum_recv, load_sem,
):
    local_x, local_y, planes = shape
    groups_x, groups_y = groups
    pad_x = (blocks.shape[1] - local_x) // 2
    pad_y = (blocks.shape[2] - local_y) // 2
    ext_x, ext_y = blocks.shape[1], blocks.shape[2]
    waves = y_fwd.shape[0] // 2
    rows = waves * ext_x
    me_x, me_y = lax.axis_index("px"), lax.axis_index("py")
    penalty = smoothing[0]
    count_x, count_y, count_z = psf_shape
    reach_x = count_x - 1

    def device(step_x, step_y):
        return {
            "px": lax.rem(me_x + step_x + groups_x, groups_x),
            "py": lax.rem(me_y + step_y + groups_y, groups_y),
        }

    barrier = pltpu.get_barrier_semaphore()
    partners = DIRECTIONS + [(0, k) for k in range(1, groups_y)] + [(k, 0) for k in range(1, groups_x)]
    for step in partners:
        pl.semaphore_signal(barrier, inc=1, device_id=device(*step), device_id_type=MESH)

    inner_x, inner_y = pl.ds(pad_x, local_x), pl.ds(pad_y, local_y)
    loads = [
        pltpu.make_async_copy(far, near, load_sem.at[number])
        for number, (far, near) in enumerate((
            (measured, blocks.at[0, inner_x, inner_y, :]),
            (z_fwd_far, z_fwd), (lap_far, lap), (z_inv_far, z_inv),
        ))
    ]
    for load in loads:
        load.start()

    def span(step, local, pad, width):
        if step == 0:
            return pl.ds(pad, local), pl.ds(pad, local)
        if step > 0:
            return pl.ds(pad + local - width, width), pl.ds(pad - width, width)
        return pl.ds(pad, width), pl.ds(pad + local, width)

    def halo(side, across):
        copies = []
        for number, (step_x, step_y) in enumerate(DIRECTIONS):
            if (step_x != 0) != across:
                continue
            from_x, to_x = span(step_x, local_x, pad_x, reach_x)
            from_y, to_y = span(step_y, local_y, pad_y, pad_y)
            copies.append(
                pltpu.make_async_remote_copy(
                    src_ref=blocks.at[side, from_x, from_y, :],
                    dst_ref=blocks.at[side, to_x, to_y, :],
                    send_sem=send_sem.at[side, number],
                    recv_sem=recv_sem.at[side, number],
                    device_id=device(step_x, step_y),
                    device_id_type=MESH,
                )
            )
        for copy in copies:
            copy.start()
        return copies

    def forward(block, beside=(), across=()):
        def lines(group):
            for k in range(4):
                x = group * 8 + 2 * k
                pair = jnp.concatenate([block[x], block[x + 1]], axis=1)
                out = dot(y_fwd[...], stack_rows(pair))
                mixed[pl.ds(x * 2 * waves, 2 * waves), :] = out[:, :planes]
                mixed[pl.ds((x + 1) * 2 * waves, 2 * waves), :] = out[:, planes:]

        for copy in beside:
            copy.wait_recv()
        pl.loop(pad_x // 8, (pad_x + local_x) // 8)(lines)
        for copy in across:
            copy.wait_recv()
        edge = pad_x // 8
        pl.loop(0, edge)(lines)
        pl.loop(ext_x // 8 - edge, ext_x // 8)(lines)

        @pl.loop(0, waves // 4)
        def _(group):
            for k in range(4):
                wave = group * 4 + k
                real = mixed[pl.ds(wave, ext_x, stride=2 * waves), :]
                imag = mixed[pl.ds(wave + waves, ext_x, stride=2 * waves), :]
                out = dot(x_fwd[...], stack_rows(jnp.concatenate([real, imag], axis=1)))
                cosine, sine = out[:ext_x], out[ext_x:]
                spectrum[pl.ds(wave * ext_x, ext_x), :planes] = cosine[:, :planes] + sine[:, planes:]
                spectrum[pl.ds(wave * ext_x, ext_x), planes:] = cosine[:, planes:] - sine[:, :planes]

    def along_z(values, table):
        high, middle, low = thirds(values)
        small = dot(low, table[0]) + dot(high, table[1])
        return dot(high, table[0]) + (dot(middle, table[0]) + small)

    chunk = rows // 2

    def apply_filter(by):
        @pl.loop(0, rows // chunk)
        def _(group):
            where = pl.ds(group * chunk, chunk)
            values = along_z(spectrum[where, :], z_fwd)
            real, imag = by(where, values[:, :planes], values[:, planes:])
            spectrum[where, :] = along_z(jnp.concatenate([real, imag], axis=1), z_inv)

    def by_power(where, real, imag):
        return real * power[where, :], imag * power[where, :]

    def by_adjoint(where, real, imag):
        re, im = adjoint[where, :planes], adjoint[where, planes:]
        return real * re + imag * im, imag * re - real * im

    def inverse(store):
        @pl.loop(0, waves // 4)
        def _(group):
            for k in range(4):
                wave = group * 4 + k
                out = dot(x_inv[...], stack_rows(spectrum[pl.ds(wave * ext_x, ext_x), :]))
                cosine, sine = out[:local_x], out[local_x:]
                back[pl.ds(wave * local_x, local_x), :] = cosine[:, :planes] - sine[:, planes:]
                back[pl.ds((wave + waves) * local_x, local_x), :] = cosine[:, planes:] + sine[:, :planes]

        @pl.loop(0, local_x // 8)
        def _(group):
            for k in range(4):
                x = group * 8 + 2 * k
                left = back[pl.ds(x, 2 * waves, stride=local_x), :]
                right = back[pl.ds(x + 1, 2 * waves, stride=local_x), :]
                out = dot(y_inv[...], stack_rows(jnp.concatenate([left, right], axis=1)))
                store(x, out[:, :planes])
                store(x + 1, out[:, planes:])

    def start_sum(slots, tile, mine, count, base, side):
        slots[side, pl.ds(mine, 1)] = tile[None]
        copies = []
        for k in range(1, count):
            copies.append(
                pltpu.make_async_remote_copy(
                    src_ref=slots.at[side, mine],
                    dst_ref=slots.at[side, mine],
                    send_sem=sum_send.at[side, base + k],
                    recv_sem=sum_recv.at[side, base + k],
                    device_id=device(0, k) if base == 0 else device(k, 0),
                    device_id_type=MESH,
                )
            )
        for copy in copies:
            copy.start()
        return copies

    def end_sum(slots, copies, side):
        for copy in copies:
            copy.wait_recv()
        tile = jnp.sum(slots[side], axis=0)
        for copy in copies:
            copy.wait_send()
        return tile

    def fold(values):
        return jnp.sum(values.reshape(-1, 8, planes), axis=0)

    def pack(gamma, delta):
        line = lax.broadcasted_iota(jnp.int32, (8, planes), 0)
        return jnp.where(
            line == 0,
            jnp.sum(gamma, axis=0, keepdims=True),
            jnp.where(line == 1, jnp.sum(delta, axis=0, keepdims=True), 0.0),
        )

    placed[...] = jnp.zeros_like(placed)
    for side in range(2):
        blocks[side, 0:pad_x - reach_x] = jnp.zeros((pad_x - reach_x, ext_y, planes), jnp.float32)
        blocks[side, ext_x - pad_x + reach_x:ext_x] = jnp.zeros((pad_x - reach_x, ext_y, planes), jnp.float32)
    unit[...] = jnp.zeros_like(unit)
    unit[:, :, 0:count_z] = psf[...] / jnp.sum(psf[...])
    origin_x, size_x = pad_x - (count_x - 1), local_x + 2 * (count_x - 1)
    origin_y, size_y = pad_y - (count_y - 1), local_y + 2 * (count_y - 1)
    half_x, half_y = count_x // 2, count_y // 2
    for low_x in range(count_x):
        at_x = origin_x + (low_x - half_x) % size_x
        turned = pltpu.roll(unit[low_x], planes - count_z // 2, 1)
        for low_y, high_y in ((0, half_y), (half_y, count_y)):
            at_y = origin_y + (low_y - half_y) % size_y
            placed[at_x, at_y:at_y + high_y - low_y, :] = turned[low_y:high_y]
    pl.semaphore_wait(barrier, len(partners))
    loads[0].wait()
    across = halo(0, True)
    beside = halo(0, False)
    forward(placed)
    loads[1].wait()
    loads[2].wait()

    @pl.loop(0, rows // chunk)
    def _(group):
        where = pl.ds(group * chunk, chunk)
        values = along_z(spectrum[where, :], z_fwd)
        adjoint[where, :] = values
        real, imag = values[:, :planes], values[:, planes:]
        power[where, :] = real * real + imag * imag + penalty * lap[where, :]

    loads[3].wait()
    forward(blocks.at[0], beside, across)
    apply_filter(by_adjoint)

    def store_right(x, values):
        blocks[1, pad_x + x, inner_y, :] = values
        residual[x] = values

    inverse(store_right)
    for copy in across + beside:
        copy.wait_send()
    across = halo(1, True)
    beside = halo(1, False)

    row = lax.broadcasted_iota(jnp.int32, (local_y, planes), 0)
    lane = lax.broadcasted_iota(jnp.int32, (local_y, planes), 1)
    edge_low_x = jnp.where(me_x == 0, penalty, 0.0)
    edge_high_x = jnp.where(me_x == groups_x - 1, penalty, 0.0)
    face_low_y = jnp.where((row == 0) & (me_y == 0), penalty, 0.0)
    face_high_y = jnp.where((row == local_y - 1) & (me_y == groups_y - 1), penalty, 0.0)
    face_low_z = jnp.where(lane == 0, penalty, 0.0)
    face_high_z = jnp.where(lane == planes - 1, penalty, 0.0)

    def operate(side, beside, across):
        forward(blocks.at[side], beside, across)
        apply_filter(by_power)

        def store_image(x, values):
            image[x] = values

        inverse(store_image)
        image[0] += edge_low_x * blocks[side, pad_x - 1, inner_y, :]
        image[local_x - 1] += edge_high_x * blocks[side, pad_x + local_x, inner_y, :]
        for copy in beside + across:
            copy.wait_send()

    def faced(side, x, here):
        below = blocks[side, pad_x + x, pl.ds(pad_y - 1, 1), :]
        above = blocks[side, pad_x + x, pl.ds(pad_y + local_y, 1), :]
        value = image[x] + face_low_y * below + face_high_y * above
        value = value + face_low_z * pltpu.roll(here, 1, 1)
        return value + face_high_z * pltpu.roll(here, planes - 1, 1)

    def sweep(low, high, line, carry):
        def some(group, carry):
            for k in range(4):
                carry = line(low + group * 4 + k, carry)
            return carry

        return lax.fori_loop(0, (high - low) // 4, some, carry)

    def sweep_and_send(line, side):
        blank = jnp.zeros((8, planes), jnp.float32)
        carry = sweep(0, pad_x, line, (blank, blank))
        carry = sweep(local_x - pad_x, local_x, line, carry)
        across = halo(side, True)
        carry = sweep(pad_x, local_x - pad_x, line, carry)
        return pack(*carry), across, halo(side, False)

    operate(1, beside, across)

    def first(x, carry):
        gamma, delta = carry
        here = blocks[1, pad_x + x, inner_y, :]
        value = faced(1, x, here)
        blocks[0, pad_x + x, inner_y, :] = value
        return gamma + fold(here * here), delta + fold(here * value)

    tile, across, beside = sweep_and_send(first, 0)

    alpha_old, gamma_old = None, None
    for count in range(ITERS):
        side = count % 2
        final = count == ITERS - 1
        copies = start_sum(sums_y, tile, me_y, groups_y, 0, side)
        tile = end_sum(sums_y, copies, side)
        copies = start_sum(sums_x, tile, me_x, groups_x, groups_y, side)
        if not final:
            operate(side, beside, across)
        sums = jnp.sum(end_sum(sums_x, copies, side), axis=1, keepdims=True)
        gamma, delta = sums[0:1], sums[1:2]
        if count == 0:
            beta = jnp.zeros((1, 1), jnp.float32)
            alpha = gamma / delta
        else:
            beta = gamma / gamma_old
            alpha = gamma / (delta - beta * gamma / alpha_old)
        alpha_old, gamma_old = alpha, gamma
        alpha_all = jnp.broadcast_to(alpha, (local_y, planes))
        beta_all = jnp.broadcast_to(beta, (local_y, planes))

        def line(x, carry):
            held = blocks[side, pad_x + x, inner_y, :]
            here = residual[x]
            if count == 0:
                step, moved = here, held
                field[x] = alpha_all * step
            else:
                step = here + beta_all * walk[x]
                moved = held + beta_all * pull[x]
                field[x] += alpha_all * step
            after = here - alpha_all * moved
            residual[x] = after
            if final:
                return carry
            walk[x] = step
            pull[x] = moved
            turn = faced(side, x, held)
            if count > 0:
                turn = turn + beta_all * swing[x]
            swing[x] = turn
            value = held - alpha_all * turn
            blocks[1 - side, pad_x + x, inner_y, :] = value
            gamma, delta = carry
            return gamma + fold(after * after), delta + fold(after * value)

        if final:
            sweep(0, local_x, line, 0)
        elif count == ITERS - 2:
            blank = jnp.zeros((8, planes), jnp.float32)
            tile = pack(*sweep(0, local_x, line, (blank, blank)))
        else:
            tile, across, beside = sweep_and_send(line, 1 - side)


def shards(measured, spread_function, smoothing):
    local_x, local_y, planes = measured.shape
    count_x, count_y, count_z = spread_function.shape
    groups_x, groups_y = lax.axis_size("px"), lax.axis_size("py")
    tables = make_tables(local_x, local_y, planes, count_x - 1, count_y - 1)
    pad_x, pad_y = round_up(count_x - 1, 8), round_up(count_y - 1, 8)
    ext_x, ext_y = local_x + 2 * pad_x, local_y + 2 * pad_y
    waves = tables["y_forward"].shape[0] // 2
    f32 = jnp.float32
    vmem = pl.BlockSpec(memory_space=pltpu.VMEM)
    far = pl.BlockSpec(memory_space=pltpu.HBM)
    body = functools.partial(
        kernel, (local_x, local_y, planes), spread_function.shape, (groups_x, groups_y)
    )
    local = (local_x, local_y, planes)
    return pl.pallas_call(
        body,
        out_shape=[jax.ShapeDtypeStruct(local, f32)] * 2,
        in_specs=[far, vmem, pl.BlockSpec(memory_space=pltpu.SMEM)] + [vmem] * 4 + [far] * 3,
        out_specs=[vmem, vmem],
        scratch_shapes=[
            pltpu.VMEM((2, ext_x, ext_y, planes), f32),
            pltpu.VMEM((ext_x, ext_y, planes), f32),
            pltpu.VMEM((ext_x * 2 * waves, planes), f32),
            pltpu.VMEM((waves * ext_x, 2 * planes), f32),
            pltpu.VMEM((2 * waves * local_x, planes), f32),
            pltpu.VMEM(local, f32),
            pltpu.VMEM(local, f32),
            pltpu.VMEM(local, f32),
            pltpu.VMEM((waves * ext_x, planes), f32),
            pltpu.VMEM((waves * ext_x, 2 * planes), f32),
            pltpu.VMEM((2, groups_y, 8, planes), f32),
            pltpu.VMEM((2, groups_x, 8, planes), f32),
            pltpu.VMEM(local, f32),
            pltpu.VMEM((count_x, count_y, planes), f32),
            pltpu.VMEM(tables["z_forward"].shape, jnp.bfloat16),
            pltpu.VMEM(tables["z_inverse"].shape, jnp.bfloat16),
            pltpu.VMEM(tables["lap"].shape, f32),
            pltpu.SemaphoreType.DMA((2, len(DIRECTIONS))),
            pltpu.SemaphoreType.DMA((2, len(DIRECTIONS))),
            pltpu.SemaphoreType.DMA((2, groups_x + groups_y)),
            pltpu.SemaphoreType.DMA((2, groups_x + groups_y)),
            pltpu.SemaphoreType.DMA((4,)),
        ],
        compiler_params=pltpu.CompilerParams(
            collective_id=0, has_side_effects=True, vmem_limit_bytes=48 * 1024 * 1024
        ),
    )(
        measured, spread_function, smoothing,
        *[jnp.asarray(tables[name]) for name in (
            "y_forward", "x_forward", "x_inverse", "y_inverse", "z_forward", "z_inverse", "lap"
        )],
    )


def solution(mesh):
    return jax.shard_map(
        shards,
        mesh=mesh,
        in_specs=(P("px", "py", None), P(), P()),
        out_specs=(P("px", "py", None), P("px", "py", None)),
        check_vma=False,
    )
```
